256 devices in a mesh: atom: 128 (over z, y, x), chan: 2 (over core).
Axes of the slice: x: 4, y: 4, z: 8, core: 2. Of those that a mesh axis runs over, the one named last changes fastest.
Arguments:
- features: bfloat16 [128, 49, 32768], P('chan', None, 'atom'), may hold values from -6 to 6
- weights: bfloat16 [3, 7, 128, 128], P(None, None, None, 'chan'), may hold values from -2 to 2
- cotangent: bfloat16 [128, 49, 32768], P('chan', None, 'atom'), may hold values from -6 to 6
- edge_bias: float32 [8, 16, 32768], P('chan', None, 'atom'), may hold values from -5 to 5
- neighbours: int32 [16, 32768], P(None, 'atom'), may hold values from 0 to 32767, as said below
- valid_mask: int32 [16, 32768], P(None, 'atom'), may hold values from 0 to 1, as said below
Outputs:
- grad_features: bfloat16 [128, 49, 32768], P('chan', None, 'atom')
- grad_weights: float32 [3, 7, 128, 128], P(None, None, None, 'chan')
- grad_bias: float32 [8, 16, 32768], P('chan', None, 'atom')
The draws below stay inside these ranges and needn't reach their ends.
Inputs may be any that keep to these rules, and one draw needn't show every extreme that they name: neighbours[s, a] = (a + o) mod 32768 with -128 <= o <= 128; offsets of -128 and 128 both occur, and slot 0 always holds (a - 1) mod 32768. `valid_mask`: slot 0 of every atom is valid; the share of valid slots rises along the atom order from about a quarter to nearly all.
All inputs are finite; a program needn't handle non-finite values.
Results may differ from the reference program's by a relative error of at most 0.005.
The reference program's roundings to bfloat16 on the way (of `projected` and `grads`) count: a program that leaves them out, or rounds other values in their place, can miss the bound.
Values may be sent and summed in bfloat16 or wider, within the bound.
A program may use at most 128 MiB of HBM per device.

```python
import jax
import jax.numpy as jnp
from jax import lax

LMAX = 6
M = 49
C = 128
H = 8
K = 16
HALO = 128
ATOMS = 32768


def draw_neighbours(key, part):
    atom_ids = jnp.arange(ATOMS, dtype=jnp.int32)[None, :]
    slot_ids = jnp.arange(K, dtype=jnp.int32)[:, None]
    offsets = jax.random.randint(key, (K, ATOMS), -HALO, HALO + 1).astype(jnp.int32)
    offsets = jnp.where(slot_ids == 0, -1, offsets)
    offsets = jnp.where((slot_ids == 1) & (atom_ids % 8 == 0), -HALO, offsets)
    offsets = jnp.where((slot_ids == 1) & (atom_ids % 8 == 4), HALO, offsets)
    return ((atom_ids + offsets) % ATOMS).astype(jnp.int32)


def draw_valid_mask(key, part):
    atom_ids = jnp.arange(ATOMS, dtype=jnp.int32)[None, :]
    slot_ids = jnp.arange(K, dtype=jnp.int32)[:, None]
    levels = 2 + 6 * atom_ids // ATOMS
    rolled = jax.random.randint(key, (K, ATOMS), 0, 8).astype(jnp.int32)
    live_slots = jnp.where(rolled < levels, 1, 0)
    return jnp.where(slot_ids == 0, 1, live_slots).astype(jnp.int32)


def draw_weights(key, part):
    shape = (3, LMAX + 1, C, C)
    base = jax.random.normal(key, shape, jnp.float32)
    factor = jnp.array([3.0, 3.0, 1.0], jnp.float32).reshape(3, 1, 1, 1)
    values = jnp.clip(base * factor / jnp.sqrt(jnp.float32(C)), -2.0, 2.0)
    return values.astype(jnp.bfloat16)


def block_levels(own_key, extent, split, least, high):
    def one(axis_at, blocks):
        draws = jax.random.uniform(jax.random.fold_in(jax.random.fold_in(own_key, 6), axis_at), (blocks,), jnp.float32, least / len(split), high / len(split))
        return jnp.repeat(jnp.exp(draws), extent[axis_at] // blocks).reshape((-1,) + (1,) * (len(extent) - axis_at - 1))

    level = one(*split[0])
    for cut in split[1:]:
        level = level * one(*cut)
    return level


def scatter_about(own_key, extent, deviation, reach, split=(), kind=jnp.bfloat16):
    result = deviation * jax.random.normal(own_key, extent, jnp.float32)
    if split:
        result = result * block_levels(own_key, extent, split, -0.22, 0.18)
    return jnp.clip(result, -reach, reach).astype(kind)


def setup_inputs(seed: int = 0) -> dict:
    key_of = jax.random.split(jax.random.key(seed), 7)
    return {
        "features": scatter_about(key_of[0], (C, M, ATOMS), 1.0, 6.0, ((0, 2), (2, 128))),
        "weights": draw_weights(jax.random.fold_in(key_of[6], 71), 0),
        "cotangent": scatter_about(key_of[2], (C, M, ATOMS), 1.0, 6.0, ((0, 2), (2, 128))),
        "edge_bias": scatter_about(key_of[3], (H, K, ATOMS), 1.0, 5.0, ((0, 2), (2, 128)), jnp.float32),
        "neighbours": draw_neighbours(jax.random.fold_in(key_of[6], 71), 0),
        "valid_mask": draw_valid_mask(jax.random.fold_in(key_of[6], 71), 0),
    }


soft_cap = 10.0


def degree_bounds():
    return [(degree * degree, (degree + 1) * (degree + 1)) for degree in range(LMAX + 1)]


def reference(features, weights, cotangent, edge_bias, neighbours, valid_mask):
    head_rows = (C // H) * M
    score_scale = 1.0 / (head_rows ** 0.5)
    feature_f = features.astype(jnp.float32)
    weight_f = weights.astype(jnp.float32)
    projected = jnp.concatenate(
        [jnp.einsum("cma,gcd->gdma", feature_f[:, low_comp:high_comp], weight_f[:, degree])
         for degree, (low_comp, high_comp) in enumerate(degree_bounds())], axis=2)
    projected = projected.astype(jnp.bfloat16)
    head_view = projected.reshape(3, H, head_rows, ATOMS)
    grad_out = cotangent.reshape(H, head_rows, ATOMS)
    live_slots = valid_mask > 0
    flat_index = neighbours.reshape(-1)

    def one_head(head_items):
        query_h, keys_h, values_h, grad_h, bias_h = head_items
        query_f = query_h.astype(jnp.float32)
        grad_f = grad_h.astype(jnp.float32)
        key_edges = keys_h[:, neighbours].astype(jnp.float32)
        value_edges = values_h[:, neighbours].astype(jnp.float32)
        raw_score = score_scale * jnp.einsum("fa,fka->ka", query_f, key_edges)
        squashed = jnp.tanh(raw_score / soft_cap)
        logits = soft_cap * squashed + bias_h
        exp_logit = jnp.where(live_slots, jnp.exp(logits), jnp.float32(0.0))
        attention = exp_logit / jnp.sum(exp_logit, axis=0, keepdims=True)
        grad_attn = jnp.einsum("fa,fka->ka", grad_f, value_edges)
        grad_logit = attention * (grad_attn - jnp.sum(attention * grad_attn, axis=0, keepdims=True))
        grad_raw = score_scale * grad_logit * (1.0 - squashed * squashed)
        grad_query = jnp.einsum("ka,fka->fa", grad_raw, key_edges)
        key_terms = (grad_raw[None] * query_f[:, None, :]).reshape(head_rows, -1)
        value_terms = (attention[None] * grad_f[:, None, :]).reshape(head_rows, -1)
        both_terms = jnp.stack([key_terms, value_terms])
        scattered = jnp.zeros((2, head_rows, ATOMS), jnp.float32).at[:, :, flat_index].add(both_terms)
        return grad_query, scattered, grad_logit

    grad_query, scattered, grad_logit = lax.map(
        one_head, (head_view[0], head_view[1], head_view[2], grad_out, edge_bias))
    grads = jnp.stack([grad_query, scattered[:, 0], scattered[:, 1]]).astype(jnp.bfloat16)
    grads_f = grads.reshape(3, C, M, ATOMS).astype(jnp.float32)
    grad_weights = jnp.stack(
        [jnp.einsum("cma,gdma->gcd", feature_f[:, low_comp:high_comp], grads_f[:, :, low_comp:high_comp])
         for low_comp, high_comp in degree_bounds()], axis=1)
    grad_features = jnp.concatenate(
        [jnp.einsum("gcd,gdma->cma", weight_f[:, degree], grads_f[:, :, low_comp:high_comp])
         for degree, (low_comp, high_comp) in enumerate(degree_bounds())], axis=1)
    return grad_features.astype(jnp.bfloat16), grad_weights, grad_logit
```

```python
import functools
import math

import jax
import jax.numpy as jnp
from jax import lax
from jax.experimental import pallas as pl
from jax.experimental.pallas import tpu as pltpu
from jax.sharding import PartitionSpec as P

LMAX = 6
HALO = 128
M = 49
STEP = 7
ROUNDS = M // STEP
CAP = 10.0
MESH = pl.DeviceIdType.MESH
f32 = jnp.float32
bf16 = jnp.bfloat16
ANY = pl.BlockSpec(memory_space=pl.ANY)
VMEM = pl.BlockSpec(memory_space=pltpu.VMEM)
DMA = pltpu.SemaphoreType.DMA


def nn(a, b):
    return lax.dot_general(a, b, (((1,), (0,)), ((), ())), preferred_element_type=f32)


def nt(a, b):
    return lax.dot_general(a, b, (((1,), (1,)), ((), ())), preferred_element_type=f32)


def tn(a, b):
    return lax.dot_general(a, b, (((0,), (0,)), ((), ())), preferred_element_type=f32)


def degree_of(m):
    degree = jnp.int32(0)
    for low in range(1, LMAX + 1):
        degree = degree + (m >= low * low).astype(jnp.int32)
    return degree


def places():
    me = lax.axis_index("atom")
    chan = lax.axis_index("chan")
    count = lax.axis_size("atom")
    return me, chan, lax.rem(me + 1, count), lax.rem(me + count - 1, count), 1 - chan


def signal(sem, atom, chan):
    pl.semaphore_signal(sem, inc=1, device_id=(atom, chan), device_id_type=MESH)


def remote(src, dst, send, recv, atom, chan):
    return pltpu.make_async_remote_copy(
        src_ref=src, dst_ref=dst, send_sem=send, recv_sem=recv,
        device_id=(atom, chan), device_id_type=MESH)


def scores_kernel(feat, cot, w, q_out, k_out, fx_out, cx_out, s_out,
                  fx, cx, q, k, v, s,
                  loc_sem, out_sem, ps, pr, hs, hr, fs, fr, cs, cr):
    me, chan, right, left, other = places()
    cl = feat.shape[1]
    rows = pl.ds(pl.multiple_of(chan * cl, cl), cl)
    halves = (slice(0, HALO), slice(HALO, 2 * HALO))

    barrier = pltpu.get_barrier_semaphore()
    signal(barrier, left, chan)
    signal(barrier, right, chan)
    signal(barrier, me, other)
    own = pltpu.make_async_copy(feat, fx.at[0, :, rows, :], loc_sem.at[0])
    own.start()
    own_cot = pltpu.make_async_copy(cot, cx.at[0], loc_sem.at[1])
    own_cot.start()
    pl.semaphore_wait(barrier, 3)

    def part(i):
        return pl.ds(STEP * i, STEP)

    halo, fwd, mate = [], [], []
    for i in range(ROUNDS):
        for d, (to, src) in enumerate(((right, halves[1]), (left, halves[0]))):
            copy = remote(feat.at[part(i), :, src], fx.at[1, part(i), rows, halves[d]],
                          hs.at[d, i], hr.at[d, i], to, chan)
            copy.start()
            halo.append(copy)
            here = fx.at[1, part(i), rows, halves[d]]
            fwd.append(remote(here, here, fs.at[d, i], fr.at[d, i], me, other))
        copy = remote(feat.at[part(i)], fx.at[0, part(i), rows, :], ps.at[i], pr.at[i], me, other)
        copy.start()
        mate.append(copy)
    border = []
    for d, (to, src) in enumerate(((right, halves[1]), (left, halves[0]))):
        copy = remote(cot.at[:, :, src], cx.at[1, :, :, halves[d]], cs.at[d], cr.at[d], to, chan)
        copy.start()
        border.append(copy)

    def project(side, i):
        for u in range(STEP):
            m = STEP * i + u
            degree = math.isqrt(m)
            weight = w[:, degree].reshape(3 * cl, 2 * cl)
            out = nn(weight, fx[side, m]).astype(bf16)
            q[side, m] = out[:cl]
            k[side, m] = out[cl:2 * cl]
            v[side, m] = out[2 * cl:]

    def head(ref, side, h):
        return ref[side, :, 16 * h:16 * h + 16, :].reshape(16 * M, 2 * HALO)

    own.wait()
    for i in range(ROUNDS):
        mate[i].wait_recv()
        project(0, i)
    own_cot.wait()
    for h in range(4):
        s[h, :, 0:2 * HALO] = tn(head(q, 0, h), head(k, 0, h))
        s[4 + h, :, 0:2 * HALO] = tn(head(cx, 0, h), head(v, 0, h))
    outs = [pltpu.make_async_copy(fx.at[0], fx_out, out_sem.at[0])]
    outs[0].start()
    for i in range(ROUNDS):
        for d in range(2):
            halo[2 * i + d].wait_recv()
            fwd[2 * i + d].start()
        if i:
            for d in range(2):
                fwd[2 * i - 2 + d].wait_recv()
            project(1, i - 1)
    for d in range(2):
        fwd[2 * ROUNDS - 2 + d].wait_recv()
    project(1, ROUNDS - 1)
    outs.append(pltpu.make_async_copy(q, q_out, out_sem.at[1]))
    outs[1].start()
    outs.append(pltpu.make_async_copy(k, k_out, out_sem.at[2]))
    outs[2].start()
    for h in range(4):
        for row, left_ref, right_ref in ((h, q, k), (4 + h, cx, v)):
            a, b = head(left_ref, 0, h), head(right_ref, 1, h)
            for side in halves:
                s[row, side, 2 * HALO:] = tn(a[:, side], b[:, side])
    outs.append(pltpu.make_async_copy(s, s_out, out_sem.at[3]))
    outs[3].start()
    for copy in border:
        copy.wait_recv()
    outs.append(pltpu.make_async_copy(cx, cx_out, out_sem.at[4]))
    outs[4].start()
    for copy in halo + fwd + mate + border:
        copy.wait_send()
    for copy in outs:
        copy.wait()


def slots_kernel(s, bias, near, valid, grad_bias, band):
    heads, slots, atoms = bias.shape
    total = atoms * lax.axis_size("atom")
    scale = 1.0 / math.sqrt(16 * M)
    first = lax.axis_index("atom") * atoms
    t = near[...] - first + HALO
    t = jnp.where(t < 0, t + total, t)
    t = jnp.where(t >= total, t - total, t)
    j = t - HALO
    pos = jnp.where(j < 0, j + atoms + HALO, j)
    pos_t = jnp.concatenate([pos] * (2 * heads), axis=0).T
    block = pos_t // HALO
    lane = pos_t - block * HALO
    which = lax.broadcasted_iota(jnp.int32, pos_t.shape, 1) // slots
    picked = jnp.zeros(pos_t.shape, f32)
    for row in range(2 * heads):
        got = [jnp.take_along_axis(s[row, :, HALO * b:HALO * (b + 1)], lane, axis=1,
                                   mode="promise_in_bounds") for b in range(3)]
        got = jnp.where(block == 0, got[0], jnp.where(block == 1, got[1], got[2]))
        picked = jnp.where(which == row, got, picked)
    picked = picked.T
    live = valid[...] > 0
    raws, attns = [], []
    for h in range(heads):
        raw = scale * picked[slots * h:slots * (h + 1)]
        grad_attn = picked[slots * (heads + h):slots * (heads + h + 1)]
        squashed = jnp.tanh(raw / CAP)
        e = jnp.where(live, jnp.exp(CAP * squashed + bias[h]), 0.0)
        attn = e / jnp.sum(e, axis=0, keepdims=True)
        grad = attn * (grad_attn - jnp.sum(attn * grad_attn, axis=0, keepdims=True))
        grad_bias[h] = grad
        raws.append(scale * grad * (1.0 - squashed * squashed))
        attns.append(attn)
    parts = raws + attns
    sums = [jnp.zeros_like(x) for x in parts]
    for t in range(slots):
        same = pos == pos[t:t + 1]
        sums = [a + jnp.where(same, x[t:t + 1], 0.0) for a, x in zip(sums, parts)]
    spread = jnp.concatenate(sums, axis=0).T
    for b in range(3):
        here = lax.broadcasted_iota(jnp.int32, (atoms, HALO), 1) + HALO * b
        slot = jnp.full((atoms, HALO), -1, jnp.int32)
        for t in range(slots):
            slot = jnp.where(pos_t[:, t:t + 1] == here, t, slot)
        there = slot >= 0
        slot = jnp.maximum(slot, 0)
        cols = slice(HALO * b, HALO * (b + 1))
        for row in range(2 * heads):
            x = jnp.take_along_axis(spread, slot + slots * row, axis=1, mode="promise_in_bounds")
            x = jnp.where(there, x, 0.0)
            hi = x.astype(bf16)
            if row < heads:
                band[row, :, cols] = hi
                band[heads + row, :, cols] = (x - hi.astype(f32)).astype(bf16)
            else:
                band[heads + row, :, cols] = hi


def grads_kernel(band, q_in, k_in, cx_in, fx_in, w, gf, gw_out,
                 p, pr, q, k, cx, fx, g, wc, gw, part, arrived,
                 loc_sem, out_sem, bs, br, ms, mr):
    me, chan, right, left, other = places()
    cl = gf.shape[1]
    halves = (slice(0, HALO), slice(HALO, 2 * HALO))
    edge = slice(2 * HALO, 3 * HALO)
    loads = [pltpu.make_async_copy(src, dst, loc_sem.at[i]) for i, (src, dst) in enumerate(
        ((band, p), (k_in, k), (q_in, q), (cx_in, cx), (fx_in, fx)))]
    for copy in loads:
        copy.start()
    barrier = pltpu.get_barrier_semaphore()
    signal(barrier, left, chan)
    signal(barrier, right, chan)
    signal(barrier, me, other)
    pl.semaphore_wait(barrier, 3)
    border = []
    for d, (to, src) in enumerate(((right, halves[1]), (left, halves[0]))):
        copy = remote(band.at[:, src, edge], pr.at[d], bs.at[d], br.at[d], to, chan)
        copy.start()
        border.append(copy)
    for degree in range(LMAX + 1):
        wc[degree] = w[:, degree].reshape(3 * cl, 2 * cl).T
    gw[...] = jnp.zeros_like(gw)

    def head(ref, side, h):
        return ref[side, :, 16 * h:16 * h + 16, :].reshape(16 * M, 2 * HALO)

    def put(kind, h, value):
        first = kind * cl + 16 * h
        g[:, first:first + 16, :] = value.astype(bf16).reshape(M, 16, 2 * HALO)

    loads[0].wait()
    loads[1].wait()
    for h in range(4):
        own, rim = head(k, 0, h), head(k, 1, h)
        total = nt(own, p[h, :, 0:2 * HALO]) + nt(own, p[4 + h, :, 0:2 * HALO])
        sides = [nt(rim[:, side], p[h, side, edge]) + nt(rim[:, side], p[4 + h, side, edge])
                 for side in halves]
        put(0, h, total + jnp.concatenate(sides, axis=1))
    loads[2].wait()
    loads[3].wait()
    for copy in border:
        copy.wait_recv()
    for h in range(4):
        for kind, ref, terms in ((1, q, (h, 4 + h)), (2, cx, (8 + h,))):
            own, rim = head(ref, 0, h), head(ref, 1, h)
            total = sum(nn(own, p[t, :, 0:2 * HALO]) for t in terms)
            sides = [sum(nn(rim[:, side], pr[d, t]) for t in terms)
                     for d, side in enumerate(halves)]
            put(kind, h, total + jnp.concatenate(sides, axis=1))
    loads[4].wait()
    for degree in range(LMAX + 1):
        total = None
        for m in range(degree * degree, (degree + 1) * (degree + 1)):
            term = nt(g[m], fx[m])
            total = term if total is None else total + term
        for kind in range(3):
            first = (kind * (LMAX + 1) + degree) * cl
            gw[first:first + cl, :] = total[kind * cl:(kind + 1) * cl]
    out = pltpu.make_async_copy(gw, gw_out, out_sem.at[0])
    out.start()
    theirs = pl.ds(pl.multiple_of(other * cl, cl), cl)
    mine = pl.ds(pl.multiple_of(chan * cl, cl), cl)
    mate = []
    for i in range(ROUNDS):
        for u in range(STEP):
            m = STEP * i + u
            part[m] = nn(wc[math.isqrt(m)], g[m])
        rows = pl.ds(STEP * i, STEP)
        copy = remote(part.at[rows, theirs, :], arrived.at[rows], ms.at[i], mr.at[i], me, other)
        copy.start()
        mate.append(copy)
    for i in range(ROUNDS):
        mate[i].wait_recv()
        for u in range(STEP):
            m = STEP * i + u
            gf[m] = (part[m, mine, :] + arrived[m]).astype(bf16)
    for copy in border + mate:
        copy.wait_send()
    out.wait()


def total_kernel(plane, gw, out, near, red, far, last, fin,
                 loc_sem, as_, ar, zs, zr, gs, gr):
    me, chan = lax.axis_index("atom"), lax.axis_index("chan")
    deep = lax.axis_size("atom") // plane
    size = red.shape[0]
    z, xy = me // plane, lax.rem(me, plane)
    beside = [lax.rem(xy + d, plane) for d in range(plane)]
    behind = [lax.rem(z + d, deep) for d in range(deep)]

    def rows(i):
        return pl.ds(pl.multiple_of(i * size, 8), size)

    barrier = pltpu.get_barrier_semaphore()
    for d in range(1, plane):
        signal(barrier, z * plane + beside[d], chan)
    for d in range(1, deep):
        signal(barrier, behind[d] * plane + xy, chan)
    own = pltpu.make_async_copy(gw.at[rows(xy)], near.at[xy], loc_sem.at[0])
    own.start()
    pl.semaphore_wait(barrier, plane + deep - 2)
    first = []
    for d in range(1, plane):
        copy = remote(gw.at[rows(beside[d])], near.at[xy], as_.at[d], ar.at[d],
                      z * plane + beside[d], chan)
        copy.start()
        first.append(copy)
    own.wait()
    for copy in first:
        copy.wait_recv()
    total = near[0]
    for i in range(1, plane):
        total = total + near[i]
    red[...] = total
    second = []
    for d in range(1, deep):
        copy = remote(red, far.at[z], zs.at[d], zr.at[d], behind[d] * plane + xy, chan)
        copy.start()
        second.append(copy)
    far[z] = total
    for copy in second:
        copy.wait_recv()
    total = far[0]
    for i in range(1, deep):
        total = total + far[i]
    last[...] = total
    third = []
    for d in range(1, plane):
        copy = remote(last, fin.at[rows(xy)], gs.at[d], gr.at[d], z * plane + beside[d], chan)
        copy.start()
        third.append(copy)
    fin[rows(xy)] = total
    for copy in third:
        copy.wait_recv()
    for copy in first + second + third:
        copy.wait_send()
    out[...] = fin[0:out.shape[0]]


def params(collective=None, limit=60):
    more = {} if collective is None else {"collective_id": collective, "has_side_effects": True}
    return pltpu.CompilerParams(vmem_limit_bytes=limit * 1024 * 1024, **more)


def on_device(features, weights, cotangent, edge_bias, neighbours, valid_mask):
    cl, _, atoms = features.shape
    heads, slots, _ = edge_bias.shape
    feat = jnp.transpose(features, (1, 0, 2))
    cot = jnp.transpose(cotangent, (1, 0, 2))
    w = jnp.transpose(weights, (0, 1, 3, 2))
    S = jax.ShapeDtypeStruct
    both = (2, M, cl, atoms)
    wide = atoms + HALO
    q, k, fx, cx, s = pl.pallas_call(
        scores_kernel,
        out_shape=(S(both, bf16), S(both, bf16), S((M, 2 * cl, atoms), bf16), S(both, bf16),
                   S((2 * heads, atoms, wide), f32)),
        in_specs=[ANY, ANY, VMEM],
        out_specs=(ANY,) * 5,
        scratch_shapes=[
            pltpu.VMEM((2, M, 2 * cl, atoms), bf16), pltpu.VMEM(both, bf16),
            pltpu.VMEM(both, bf16), pltpu.VMEM(both, bf16), pltpu.VMEM(both, bf16),
            pltpu.VMEM((2 * heads, atoms, wide), f32),
            DMA((2,)), DMA((5,)), DMA((ROUNDS,)), DMA((ROUNDS,)),
            DMA((2, ROUNDS)), DMA((2, ROUNDS)), DMA((2, ROUNDS)), DMA((2, ROUNDS)),
            DMA((2,)), DMA((2,))],
        compiler_params=params(0), name="scores",
    )(feat, cot, w)
    grad_bias, band = pl.pallas_call(
        slots_kernel,
        out_shape=(S(edge_bias.shape, f32), S((3 * heads, atoms, wide), bf16)),
        in_specs=[VMEM] * 4,
        out_specs=(VMEM, VMEM),
        compiler_params=params(), name="slots",
    )(s, edge_bias, neighbours, valid_mask)
    kinds = 3 * (LMAX + 1) * cl
    plane = 16
    size = -(-kinds // (8 * plane)) * 8
    gf, gw = pl.pallas_call(
        grads_kernel,
        out_shape=(S((M, cl, atoms), bf16), S((plane * size, 2 * cl), f32)),
        in_specs=[ANY] * 5 + [VMEM],
        out_specs=(VMEM, ANY),
        scratch_shapes=[
            pltpu.VMEM((3 * heads, atoms, wide), bf16), pltpu.VMEM((2, 3 * heads, HALO, HALO), bf16),
            pltpu.VMEM(both, bf16), pltpu.VMEM(both, bf16), pltpu.VMEM(both, bf16),
            pltpu.VMEM((M, 2 * cl, atoms), bf16), pltpu.VMEM((M, 3 * cl, atoms), bf16),
            pltpu.VMEM((LMAX + 1, 2 * cl, 3 * cl), bf16), pltpu.VMEM((plane * size, 2 * cl), f32),
            pltpu.VMEM((M, 2 * cl, atoms), f32), pltpu.VMEM((M, cl, atoms), f32),
            DMA((5,)), DMA((1,)), DMA((2,)), DMA((2,)), DMA((ROUNDS,)), DMA((ROUNDS,))],
        compiler_params=params(1), name="grads",
    )(band, q, k, cx, fx, w)
    deep = lax.axis_size("atom") // plane
    total = pl.pallas_call(
        functools.partial(total_kernel, plane),
        out_shape=S((kinds, 2 * cl), f32),
        in_specs=[ANY],
        out_specs=VMEM,
        scratch_shapes=[
            pltpu.VMEM((plane, size, 2 * cl), f32), pltpu.VMEM((size, 2 * cl), f32),
            pltpu.VMEM((deep, size, 2 * cl), f32), pltpu.VMEM((size, 2 * cl), f32),
            pltpu.VMEM((plane * size, 2 * cl), f32),
            DMA((1,)), DMA((plane,)), DMA((plane,)), DMA((deep,)), DMA((deep,)),
            DMA((plane,)), DMA((plane,))],
        compiler_params=params(2, 16), name="total",
    )(gw)
    grad_weights = jnp.transpose(total.reshape(3, LMAX + 1, cl, 2 * cl), (0, 1, 3, 2))
    return jnp.transpose(gf, (1, 0, 2)), grad_weights, grad_bias


def solution(mesh):
    return jax.shard_map(
        on_device,
        mesh=mesh,
        in_specs=(P("chan", None, "atom"), P(None, None, None, "chan"), P("chan", None, "atom"),
                  P("chan", None, "atom"), P(None, "atom"), P(None, "atom")),
        out_specs=(P("chan", None, "atom"), P(None, None, None, "chan"), P("chan", None, "atom")),
        check_vma=False,
    )
```

```python
import functools
import math

import jax
import jax.numpy as jnp
from jax import lax
from jax.experimental import pallas as pl
from jax.experimental.pallas import tpu as pltpu
from jax.sharding import PartitionSpec as P

LMAX = 6
HALO = 128
M = 49
STEP = 7
ROUNDS = M // STEP
CAP = 10.0
MESH = pl.DeviceIdType.MESH
f32 = jnp.float32
bf16 = jnp.bfloat16
ANY = pl.BlockSpec(memory_space=pl.ANY)
VMEM = pl.BlockSpec(memory_space=pltpu.VMEM)
DMA = pltpu.SemaphoreType.DMA


def nn(a, b):
    return lax.dot_general(a, b, (((1,), (0,)), ((), ())), preferred_element_type=f32)


def nt(a, b):
    return lax.dot_general(a, b, (((1,), (1,)), ((), ())), preferred_element_type=f32)


def tn(a, b):
    return lax.dot_general(a, b, (((0,), (0,)), ((), ())), preferred_element_type=f32)


def places():
    me = lax.axis_index("atom")
    chan = lax.axis_index("chan")
    count = lax.axis_size("atom")
    return me, chan, lax.rem(me + 1, count), lax.rem(me + count - 1, count), 1 - chan


def signal(sem, atom, chan):
    pl.semaphore_signal(sem, inc=1, device_id=(atom, chan), device_id_type=MESH)


def remote(src, dst, send, recv, atom, chan):
    return pltpu.make_async_remote_copy(
        src_ref=src, dst_ref=dst, send_sem=send, recv_sem=recv,
        device_id=(atom, chan), device_id_type=MESH)


def layer_kernel(plane, feat, cot, w, bias, near, valid, gf_out, gw_out, grad_bias,
                 fx, cx, q, k, v, s, nx, spread, xs, p, pr, g, part, arrived, gf, wc, gw,
                 a_near, a_red, a_far, a_last, b_near, b_red, b_far, b_last, fin,
                 loc_sem, out_sem, ns, nr, ps, pr_sem, hs, hr, fs, fr, cs, cr, xss, xsr, ms, mr,
                 a1s, a1r, a2s, a2r, a3s, a3r, b1s, b1r, b2s, b2r, b3s, b3r):
    me, chan, right, left, other = places()
    heads, slots, atoms = bias.shape
    cl = feat.shape[1]
    count = lax.axis_size("atom")
    deep = count // plane
    z, xy = me // plane, lax.rem(me, plane)
    beside = [z * plane + lax.rem(xy + d, plane) for d in range(plane)]
    behind = [lax.rem(z + d, deep) * plane + xy for d in range(deep)]
    size = a_red.shape[0]
    rows = pl.ds(pl.multiple_of(chan * cl, cl), cl)
    theirs = pl.ds(pl.multiple_of(other * cl, cl), cl)
    halves = (slice(0, HALO), slice(HALO, 2 * HALO))
    edge = slice(2 * HALO, 3 * HALO)
    ways = ((right, halves[1]), (left, halves[0]))

    def piece(i, base=0):
        return pl.ds(pl.multiple_of(base + i * size, 8), size)

    def chunk(i):
        return pl.ds(STEP * i, STEP)

    def head(ref, side, h):
        return ref[side, :, 16 * h:16 * h + 16, :].reshape(16 * M, 2 * HALO)

    barrier = pltpu.get_barrier_semaphore()
    signal(barrier, left, chan)
    signal(barrier, right, chan)
    signal(barrier, me, other)
    for peer in beside[1:] + behind[1:]:
        signal(barrier, peer, chan)
    own = pltpu.make_async_copy(feat, fx.at[0, :, rows, :], loc_sem.at[0])
    own.start()
    own_cot = pltpu.make_async_copy(cot, cx.at[0], loc_sem.at[1])
    own_cot.start()
    for degree in range(LMAX + 1):
        wc[degree] = w[:, degree].reshape(3 * cl, 2 * cl).T
    pl.semaphore_wait(barrier, plane + deep + 1)

    sent = []

    def go(copy):
        copy.start()
        sent.append(copy)
        return copy

    table = [go(remote(near.at[:, src], nx.at[d], ns.at[d], nr.at[d], to, chan))
             for d, (to, src) in enumerate(ways)]
    halo, fwd, mate = [], [], []
    for i in range(ROUNDS):
        for d, (to, src) in enumerate(ways):
            here = fx.at[1, chunk(i), rows, halves[d]]
            halo.append(go(remote(feat.at[chunk(i), :, src], here, hs.at[d, i], hr.at[d, i],
                                  to, chan)))
            fwd.append(remote(here, here, fs.at[d, i], fr.at[d, i], me, other))
        mate.append(go(remote(feat.at[chunk(i)], fx.at[0, chunk(i), rows, :],
                              ps.at[i], pr_sem.at[i], me, other)))
    cuts = (slice(0, 28), slice(28, M))

    def send_cot(n):
        return [go(remote(cot.at[cuts[n], :, src], cx.at[1, cuts[n], :, halves[d]],
                          cs.at[d, n], cr.at[d, n], to, chan))
                for d, (to, src) in enumerate(ways)]

    border = send_cot(0)

    def project(side, i):
        for u in range(STEP):
            m = STEP * i + u
            weight = w[:, math.isqrt(m)].reshape(3 * cl, 2 * cl)
            out = nn(weight, fx[side, m]).astype(bf16)
            q[side, m] = out[:cl]
            k[side, m] = out[cl:2 * cl]
            v[side, m] = out[2 * cl:]

    own.wait()
    for i in range(ROUNDS):
        mate[i].wait_recv()
        project(0, i)
    own_cot.wait()
    for h in range(heads):
        s[h, :, 0:atoms] = tn(head(q, 0, h), head(k, 0, h))
        s[heads + h, :, 0:atoms] = tn(head(cx, 0, h), head(v, 0, h))

    total = atoms * count
    first = me * atoms

    def local(x):
        t = x - first + HALO
        t = jnp.where(t < 0, t + total, t)
        return jnp.where(t >= total, t - total, t) - HALO

    def turned(x):
        return jnp.concatenate([x] * (2 * heads), axis=0).T

    def slot_of(pos_t, low):
        here = lax.broadcasted_iota(jnp.int32, (pos_t.shape[0], HALO), 1) + low
        slot = jnp.full(here.shape, -1, jnp.int32)
        for t in range(slots):
            slot = jnp.where(pos_t[:, t:t + 1] == here, t, slot)
        return slot

    def spread_out(values, slot, write):
        there = slot >= 0
        slot = jnp.maximum(slot, 0)
        for row in range(2 * heads):
            x = jnp.take_along_axis(values, slot + slots * row, axis=1,
                                    mode="promise_in_bounds")
            x = jnp.where(there, x, 0.0)
            hi = x.astype(bf16)
            write(row, hi)
            write(2 * heads + row, (x - hi.astype(f32)).astype(bf16))

    j = local(near[...])
    pos = jnp.where(j < 0, j + atoms + HALO, j)
    pos_t = turned(pos)

    for i in range(ROUNDS):
        for d in range(2):
            halo[2 * i + d].wait_recv()
            go(fwd[2 * i + d])
        if i:
            for d in range(2):
                fwd[2 * i - 2 + d].wait_recv()
            project(1, i - 1)
    for d in range(2):
        fwd[2 * ROUNDS - 2 + d].wait_recv()
    project(1, ROUNDS - 1)
    for h in range(heads):
        for row, left_ref, right_ref in ((h, q, k), (heads + h, cx, v)):
            a, b = head(left_ref, 0, h), head(right_ref, 1, h)
            for side in halves:
                s[row, side, edge] = tn(a[:, side], b[:, side])

    scale = 1.0 / math.sqrt(16 * M)
    block = pos_t // HALO
    lane = pos_t - block * HALO
    which = lax.broadcasted_iota(jnp.int32, pos_t.shape, 1) // slots
    picked = jnp.zeros(pos_t.shape, f32)
    for row in range(2 * heads):
        got = [jnp.take_along_axis(s[row, :, HALO * b:HALO * (b + 1)], lane, axis=1,
                                   mode="promise_in_bounds") for b in range(3)]
        got = jnp.where(block == 0, got[0], jnp.where(block == 1, got[1], got[2]))
        picked = jnp.where(which == row, got, picked)
    picked = picked.T
    live = valid[...] > 0
    raws, attns = [], []
    for h in range(heads):
        raw = scale * picked[slots * h:slots * (h + 1)]
        grad_attn = picked[slots * (heads + h):slots * (heads + h + 1)]
        squashed = jnp.tanh(raw / CAP)
        e = jnp.where(live, jnp.exp(CAP * squashed + bias[h]), 0.0)
        attn = e / jnp.sum(e, axis=0, keepdims=True)
        grad = attn * (grad_attn - jnp.sum(attn * grad_attn, axis=0, keepdims=True))
        grad_bias[h] = grad
        raws.append(scale * grad * (1.0 - squashed * squashed))
        attns.append(attn)
    parts = raws + attns
    sums = [jnp.zeros_like(x) for x in parts]
    for t in range(slots):
        same = pos == pos[t:t + 1]
        sums = [a + jnp.where(same, x[t:t + 1], 0.0) for a, x in zip(sums, parts)]
    spread[...] = jnp.concatenate(sums, axis=0).T
    rims = [go(remote(spread.at[src], xs.at[d], xss.at[d], xsr.at[d], to, chan))
            for d, (to, src) in enumerate(ways)]
    border += send_cot(1)

    for b in range(3):
        def write(row, x, b=b):
            p[row, :, HALO * b:HALO * (b + 1)] = x
        spread_out(spread[...], slot_of(pos_t, HALO * b), write)

    def put(kind, h, value):
        low = kind * cl + 16 * h
        g[:, low:low + 16, :] = value.astype(bf16).reshape(M, 16, atoms)

    def keep(kind, h):
        low = (kind - 1) * cl + 16 * h
        return slice(low, low + 16)

    for h in range(heads):
        mine, rim = head(k, 0, h), head(k, 1, h)
        terms = (h, 2 * heads + h)
        inner = sum(nt(mine, p[t, :, 0:atoms]) for t in terms)
        sides = [sum(nt(rim[:, side], p[t, side, edge]) for t in terms) for side in halves]
        put(0, h, inner + jnp.concatenate(sides, axis=1))
    for degree in range(LMAX + 1):
        acc = None
        for m in range(degree * degree, (degree + 1) * (degree + 1)):
            term = nt(g[m, 0:cl], fx[0, m])
            acc = term if acc is None else acc + term
        gw[degree * cl:(degree + 1) * cl, :] = acc
    b_one = []
    for d in range(1, deep):
        to = lax.rem(z + d, deep)
        b_one.append(go(remote(gw.at[piece(to)], b_near.at[z], b1s.at[d], b1r.at[d],
                               behind[d], chan)))
    b_near[z] = gw[piece(z)]
    for h in range(heads):
        for kind, ref in ((1, q), (2, cx)):
            mine = head(ref, 0, h)
            base = (kind - 1) * heads + h
            inner = sum(nn(mine, p[t, :, 0:atoms]) for t in (base, 2 * heads + base))
            part[:, keep(kind, h), :] = inner.reshape(M, 16, atoms)
    for d in range(2):
        table[d].wait_recv()
        rims[d].wait_recv()

        def write(row, x, d=d):
            pr[d, row] = x
        spread_out(xs[d], slot_of(turned(local(nx[d])), HALO * d), write)

    def finish(kind, ref):
        for h in range(heads):
            rim = head(ref, 1, h)
            base = (kind - 1) * heads + h
            sides = [sum(nn(rim[:, side], pr[d, t]) for t in (base, 2 * heads + base))
                     for d, side in enumerate(halves)]
            inner = part[:, keep(kind, h), :].reshape(16 * M, atoms)
            put(kind, h, inner + jnp.concatenate(sides, axis=1))

    finish(1, q)
    for copy in border:
        copy.wait_recv()
    finish(2, cx)
    for copy in b_one:
        copy.wait_recv()
    b_red[...] = sum(b_near[i] for i in range(deep))
    b_two = [go(remote(b_red, b_far.at[xy], b2s.at[d], b2r.at[d], beside[d], chan))
             for d in range(1, plane)]
    b_far[xy] = b_red[...]
    kinds = LMAX + 1
    for degree in range(kinds):
        acc = None
        for m in range(degree * degree, (degree + 1) * (degree + 1)):
            term = nt(g[m, cl:3 * cl], fx[0, m])
            acc = term if acc is None else acc + term
        for kind in (1, 2):
            low = (kind * kinds + degree) * cl
            gw[low:low + cl, :] = acc[(kind - 1) * cl:kind * cl]
    base = kinds * cl
    a_one = []
    for d in range(1, plane):
        to = lax.rem(xy + d, plane)
        a_one.append(go(remote(gw.at[piece(to, base)], a_near.at[xy], a1s.at[d], a1r.at[d],
                               beside[d], chan)))
    a_near[xy] = gw[piece(xy, base)]

    def feature_terms(i):
        for u in range(STEP):
            m = STEP * i + u
            part[m] = nn(wc[math.isqrt(m)], g[m])
        return go(remote(part.at[chunk(i), theirs, :], arrived.at[chunk(i)],
                         ms.at[i], mr.at[i], me, other))

    swap = [feature_terms(i) for i in range(ROUNDS)]
    for copy in a_one:
        copy.wait_recv()
    a_red[...] = sum(a_near[i] for i in range(plane))
    a_two = [go(remote(a_red, a_far.at[z], a2s.at[d], a2r.at[d], behind[d], chan))
             for d in range(1, deep)]
    a_far[z] = a_red[...]
    for copy in b_two:
        copy.wait_recv()
    b_last[...] = sum(b_far[i] for i in range(plane))
    b_three = [go(remote(b_last, fin.at[piece(z)], b3s.at[d], b3r.at[d], behind[d], chan))
               for d in range(1, deep)]
    fin[piece(z)] = b_last[...]
    for i in range(2):
        swap[i].wait_recv()
    for copy in a_two:
        copy.wait_recv()
    a_last[...] = sum(a_far[i] for i in range(deep))
    a_three = [go(remote(a_last, fin.at[piece(xy, base)], a3s.at[d], a3r.at[d], beside[d], chan))
               for d in range(1, plane)]
    fin[piece(xy, base)] = a_last[...]
    outs = []
    for i in range(ROUNDS):
        if i > 1:
            swap[i].wait_recv()
        for u in range(STEP):
            m = STEP * i + u
            gf[m] = (part[m, rows, :] + arrived[m]).astype(bf16)
        outs.append(pltpu.make_async_copy(gf.at[chunk(i)], gf_out.at[chunk(i)], out_sem.at[i]))
        outs[i].start()
    for copy in b_three + a_three:
        copy.wait_recv()
    gw_out[...] = fin[...]
    for copy in sent:
        copy.wait_send()
    for copy in outs:
        copy.wait()


def on_device(features, weights, cotangent, edge_bias, neighbours, valid_mask):
    cl, _, atoms = features.shape
    heads, slots, _ = edge_bias.shape
    feat = jnp.transpose(features, (1, 0, 2))
    cot = jnp.transpose(cotangent, (1, 0, 2))
    w = jnp.transpose(weights, (0, 1, 3, 2))
    S = jax.ShapeDtypeStruct
    both = (2, M, cl, atoms)
    wide = atoms + HALO
    kinds = 3 * (LMAX + 1) * cl
    plane = 16
    deep = lax.axis_size("atom") // plane
    size = (LMAX + 1) * cl // deep
    V = pltpu.VMEM
    row = (size, 2 * cl)
    gf, total, grad_bias = pl.pallas_call(
        functools.partial(layer_kernel, plane),
        out_shape=(S((M, cl, atoms), bf16), S((kinds, 2 * cl), f32), S(edge_bias.shape, f32)),
        in_specs=[ANY, ANY, VMEM, VMEM, VMEM, VMEM],
        out_specs=(ANY, VMEM, VMEM),
        scratch_shapes=[
            V((2, M, 2 * cl, atoms), bf16), V(both, bf16), V(both, bf16), V(both, bf16),
            V(both, bf16), V((2 * heads, atoms, wide), f32), V((2, slots, HALO), jnp.int32),
            V((atoms, HALO), f32), V((2, HALO, HALO), f32),
            V((4 * heads, atoms, wide), bf16), V((2, 4 * heads, HALO, HALO), bf16),
            V((M, 3 * cl, atoms), bf16), V((M, 2 * cl, atoms), f32), V((M, cl, atoms), f32),
            V((M, cl, atoms), bf16), V((LMAX + 1, 2 * cl, 3 * cl), bf16), V((kinds, 2 * cl), f32),
            V((plane, *row), f32), V(row, f32), V((deep, *row), f32), V(row, f32),
            V((deep, *row), f32), V(row, f32), V((plane, *row), f32), V(row, f32),
            V((kinds, 2 * cl), f32),
            DMA((2,)), DMA((ROUNDS,)), DMA((2,)), DMA((2,)), DMA((ROUNDS,)), DMA((ROUNDS,)),
            DMA((2, ROUNDS)), DMA((2, ROUNDS)), DMA((2, ROUNDS)), DMA((2, ROUNDS)),
            DMA((2, 2)), DMA((2, 2)), DMA((2,)), DMA((2,)), DMA((ROUNDS,)), DMA((ROUNDS,)),
            DMA((plane,)), DMA((plane,)), DMA((deep,)), DMA((deep,)), DMA((plane,)), DMA((plane,)),
            DMA((deep,)), DMA((deep,)), DMA((plane,)), DMA((plane,)), DMA((deep,)), DMA((deep,))],
        compiler_params=pltpu.CompilerParams(
            vmem_limit_bytes=62 * 1024 * 1024, collective_id=0, has_side_effects=True),
        name="layer",
    )(feat, cot, w, edge_bias, neighbours, valid_mask)
    grad_weights = jnp.transpose(total.reshape(3, LMAX + 1, cl, 2 * cl), (0, 1, 3, 2))
    return jnp.transpose(gf, (1, 0, 2)), grad_weights, grad_bias


def solution(mesh):
    return jax.shard_map(
        on_device,
        mesh=mesh,
        in_specs=(P("chan", None, "atom"), P(None, None, None, "chan"), P("chan", None, "atom"),
                  P("chan", None, "atom"), P(None, "atom"), P(None, "atom")),
        out_specs=(P("chan", None, "atom"), P(None, None, None, "chan"), P("chan", None, "atom")),
        check_vma=False,
    )
```

```python
import functools
import math

import jax
import jax.numpy as jnp
from jax import lax
from jax.experimental import pallas as pl
from jax.experimental.pallas import tpu as pltpu
from jax.sharding import PartitionSpec as P

LMAX = 6
HALO = 128
M = 49
STEP = 7
ROUNDS = M // STEP
CAP = 10.0
MESH = pl.DeviceIdType.MESH
f32 = jnp.float32
bf16 = jnp.bfloat16
ANY = pl.BlockSpec(memory_space=pl.ANY)
VMEM = pl.BlockSpec(memory_space=pltpu.VMEM)
DMA = pltpu.SemaphoreType.DMA


def nn(a, b):
    return lax.dot_general(a, b, (((1,), (0,)), ((), ())), preferred_element_type=f32)


def nt(a, b):
    return lax.dot_general(a, b, (((1,), (1,)), ((), ())), preferred_element_type=f32)


def tn(a, b):
    return lax.dot_general(a, b, (((0,), (0,)), ((), ())), preferred_element_type=f32)


def places():
    me = lax.axis_index("atom")
    chan = lax.axis_index("chan")
    count = lax.axis_size("atom")
    return me, chan, lax.rem(me + 1, count), lax.rem(me + count - 1, count), 1 - chan


def signal(sem, atom, chan):
    pl.semaphore_signal(sem, inc=1, device_id=(atom, chan), device_id_type=MESH)


def remote(src, dst, send, recv, atom, chan):
    return pltpu.make_async_remote_copy(
        src_ref=src, dst_ref=dst, send_sem=send, recv_sem=recv,
        device_id=(atom, chan), device_id_type=MESH)


def layer_kernel(plane, feat, cot, w, bias, near, valid, gf_out, gw_out, grad_bias,
                 fx, cx, q, k, v, s, nx, spread, xs, slot_own, slot_rim, p, pr, g, part, arrived,
                 gf, wc, gw, a_near, a_red, a_far, a_last, b_near, b_red, b_far, b_last, fin,
                 loc_sem, out_sem, ns, nr, ps, pr_sem, hs, hr, fs, fr, cs, cr, xss, xsr, ms, mr,
                 a1s, a1r, a2s, a2r, a3s, a3r, b1s, b1r, b2s, b2r, b3s, b3r):
    me, chan, right, left, other = places()
    heads, slots, atoms = bias.shape
    cl = feat.shape[1]
    count = lax.axis_size("atom")
    deep = count // plane
    z, xy = me // plane, lax.rem(me, plane)
    beside = [z * plane + lax.rem(xy + d, plane) for d in range(plane)]
    behind = [lax.rem(z + d, deep) * plane + xy for d in range(deep)]
    rows = pl.ds(pl.multiple_of(chan * cl, cl), cl)
    theirs = pl.ds(pl.multiple_of(other * cl, cl), cl)
    halves = (slice(0, HALO), slice(HALO, 2 * HALO))
    edge = slice(2 * HALO, 3 * HALO)
    ways = ((right, halves[1]), (left, halves[0]))

    def chunk(i):
        return pl.ds(STEP * i, STEP)

    def head(ref, side, h):
        return ref[side, :, 16 * h:16 * h + 16, :].reshape(16 * M, 2 * HALO)

    barrier = pltpu.get_barrier_semaphore()
    signal(barrier, left, chan)
    signal(barrier, right, chan)
    signal(barrier, me, other)
    for peer in beside[1:] + behind[1:]:
        signal(barrier, peer, chan)
    own = pltpu.make_async_copy(feat, fx.at[0, :, rows, :], loc_sem.at[0])
    own.start()
    own_cot = pltpu.make_async_copy(cot, cx.at[0], loc_sem.at[1])
    own_cot.start()
    pl.semaphore_wait(barrier, plane + deep + 1)

    sent = []

    def go(copy):
        copy.start()
        sent.append(copy)
        return copy

    table = [go(remote(near.at[:, src], nx.at[d], ns.at[d], nr.at[d], to, chan))
             for d, (to, src) in enumerate(ways)]
    halo, fwd, mate, late = [], [], [], []
    for i in range(ROUNDS):
        for d, (to, src) in enumerate(ways):
            here = fx.at[1, chunk(i), rows, halves[d]]
            halo.append(remote(feat.at[chunk(i), :, src], here, hs.at[d, i], hr.at[d, i],
                               to, chan))
            fwd.append(remote(here, here, fs.at[d, i], fr.at[d, i], me, other))
    for h in range(heads):
        at = slice(16 * h, 16 * h + 16)
        for d, (to, src) in enumerate(ways):
            late.append(remote(cot.at[:, at, src], cx.at[1, :, at, halves[d]],
                               cs.at[d, h], cr.at[d, h], to, chan))
    queue = halo + late

    def feed(n):
        if n > 1:
            for copy in queue[2 * n - 4:2 * n - 2]:
                copy.wait_send()
        for copy in queue[2 * n:2 * n + 2]:
            copy.start()

    def relay(i):
        for copy in halo[2 * i:2 * i + 2]:
            copy.wait_recv()
        for copy in fwd[2 * i:2 * i + 2]:
            go(copy)

    feed(0)
    feed(1)
    for i in range(ROUNDS):
        mate.append(go(remote(feat.at[chunk(i)], fx.at[0, chunk(i), rows, :],
                              ps.at[i], pr_sem.at[i], me, other)))

    def project(side, i):
        for u in range(STEP):
            m = STEP * i + u
            weight = w[:, math.isqrt(m)].reshape(3 * cl, 2 * cl)
            out = nn(weight, fx[side, m]).astype(bf16)
            q[side, m] = out[:cl]
            k[side, m] = out[cl:2 * cl]
            v[side, m] = out[2 * cl:]

    def own_scores(h):
        s[h, :, 0:atoms] = tn(head(q, 0, h), head(k, 0, h))
        s[heads + h, :, 0:atoms] = tn(head(cx, 0, h), head(v, 0, h))

    own.wait()
    for i in range(ROUNDS):
        mate[i].wait_recv()
        project(0, i)
        if i == 3:
            feed(2)
    feed(3)
    own_cot.wait()
    own_scores(0)
    own_scores(1)
    feed(4)
    own_scores(2)
    own_scores(3)
    for degree in range(LMAX + 1):
        wc[degree] = w[:, degree].reshape(3 * cl, 2 * cl).T
    feed(5)
    relay(0)
    relay(1)

    total = atoms * count
    first = me * atoms
    strip = 64

    def local(x):
        t = x - first + HALO
        t = jnp.where(t < 0, t + total, t)
        return jnp.where(t >= total, t - total, t) - HALO

    def turned(x):
        return jnp.concatenate([x] * (2 * heads), axis=0).T

    def slot_table(pos_t, low, ref):
        for r in range(0, pos_t.shape[0], strip):
            here = lax.broadcasted_iota(jnp.int32, (strip, HALO), 1) + low
            slot = jnp.full(here.shape, -1, jnp.int32)
            for t in range(slots):
                slot = jnp.where(pos_t[r:r + strip, t:t + 1] == here, t, slot)
            ref[r:r + strip, :] = slot

    def spread_out(values, table, write):
        for r in range(0, values.shape[0], strip):
            value = values[r:r + strip, :]
            slot = table[r:r + strip, :]
            there = slot >= 0
            slot = jnp.maximum(slot, 0)
            for row in range(2 * heads):
                x = jnp.take_along_axis(value, slot + slots * row, axis=1,
                                        mode="promise_in_bounds")
                x = jnp.where(there, x, 0.0)
                hi = x.astype(bf16)
                write(row, r, hi)
                write(2 * heads + row, r, (x - hi.astype(f32)).astype(bf16))

    j = local(near[...])
    pos = jnp.where(j < 0, j + atoms + HALO, j)
    pos_t = turned(pos)
    for b in range(3):
        slot_table(pos_t, HALO * b, slot_own.at[b])
    feed(6)
    relay(2)
    relay(3)
    for d in range(2):
        table[d].wait_recv()
        slot_table(turned(local(nx[d])), HALO * d, slot_rim.at[d])
    blank = jnp.zeros((4 * heads, HALO, HALO), bf16)
    p[:, 0:HALO, 3 * HALO:] = blank
    p[:, HALO:, 2 * HALO:3 * HALO] = blank
    pr[:, 0:HALO, HALO:] = blank
    pr[:, HALO:, 0:HALO] = blank
    gw[gw_out.shape[0]:, :] = jnp.zeros((gw.shape[0] - gw_out.shape[0], 2 * cl), f32)

    def rim_project(i):
        for copy in fwd[2 * i:2 * i + 2]:
            copy.wait_recv()
        project(1, i)

    feed(7)
    for i in range(3):
        rim_project(i)
    relay(4)
    rim_project(3)
    relay(5)
    rim_project(4)
    feed(8)
    relay(6)
    rim_project(5)
    rim_project(6)
    for h in range(heads):
        for row, left_ref, right_ref in ((h, q, k), (heads + h, cx, v)):
            a, b = head(left_ref, 0, h), head(right_ref, 1, h)
            for side in halves:
                s[row, side, edge] = tn(a[:, side], b[:, side])

    scale = 1.0 / math.sqrt(16 * M)
    strips = []
    for r in range(0, atoms, strip):
        at = pos_t[r:r + strip]
        block = at // HALO
        lane = at - block * HALO
        which = lax.broadcasted_iota(jnp.int32, at.shape, 1) // slots
        picked = jnp.zeros(at.shape, f32)
        for row in range(2 * heads):
            got = [jnp.take_along_axis(s[row, r:r + strip, HALO * b:HALO * (b + 1)], lane, axis=1,
                                       mode="promise_in_bounds") for b in range(3)]
            got = jnp.where(block == 0, got[0], jnp.where(block == 1, got[1], got[2]))
            picked = jnp.where(which == row, got, picked)
        strips.append(picked)
    picked = jnp.concatenate(strips, axis=0).T
    live = valid[...] > 0
    raws, attns = [], []
    for h in range(heads):
        raw = scale * picked[slots * h:slots * (h + 1)]
        grad_attn = picked[slots * (heads + h):slots * (heads + h + 1)]
        squashed = jnp.tanh(raw / CAP)
        e = jnp.where(live, jnp.exp(CAP * squashed + bias[h]), 0.0)
        attn = e / jnp.sum(e, axis=0, keepdims=True)
        grad = attn * (grad_attn - jnp.sum(attn * grad_attn, axis=0, keepdims=True))
        grad_bias[h] = grad
        grad_raw = scale * grad * (1.0 - squashed * squashed)
        raw_sum, attn_sum = jnp.zeros_like(attn), jnp.zeros_like(attn)
        for t in range(slots):
            same = pos == pos[t:t + 1]
            raw_sum += jnp.where(same, grad_raw[t:t + 1], 0.0)
            attn_sum += jnp.where(same, attn[t:t + 1], 0.0)
        raws.append(raw_sum)
        attns.append(attn_sum)
    spread[...] = jnp.concatenate(raws + attns, axis=0).T
    rims = [go(remote(spread.at[src], xs.at[d], xss.at[d], xsr.at[d], to, chan))
            for d, (to, src) in enumerate(ways)]
    for copy in late[4:]:
        copy.start()

    for b in range(3):
        def write(row, r, x, b=b):
            low = HALO * b + (HALO if b == 2 and r >= HALO else 0)
            p[row, r:r + strip, low:low + HALO] = x
        spread_out(spread, slot_own.at[b], write)

    kinds = LMAX + 1

    def put(kind, h, value):
        low = kind * cl + 16 * h
        g[:, low:low + 16, :] = value.astype(bf16).reshape(M, 16, atoms)

    def weight_terms(kind, low, high):
        for degree in range(kinds):
            ms = range(degree * degree, (degree + 1) * (degree + 1))
            at = slice(kind * cl + low, kind * cl + high)
            acc = nt(jnp.concatenate([g[m, at] for m in ms], axis=1),
                     jnp.concatenate([fx[0, m] for m in ms], axis=1))
            for one in range(low // cl, -(-high // cl)):
                first, last = max(low, one * cl), min(high, one * cl + cl)
                to = ((kind + one) * kinds + degree) * cl
                gw[to + first - one * cl:to + last - one * cl, :] = acc[first - low:last - low]

    def reduce_steps(base, size, near_, red, far, last, sems):
        s1, r1, s2, r2, s3, r3 = sems

        def piece(i):
            return pl.ds(pl.multiple_of(base + i * size, 8), size)

        def one():
            out = [go(remote(gw.at[piece(lax.rem(xy + d, plane))], near_.at[xy], s1.at[d],
                             r1.at[d], beside[d], chan)) for d in range(1, plane)]
            near_[xy] = gw[piece(xy)]
            return out

        def two():
            red[...] = sum(near_[i] for i in range(plane))
            out = [go(remote(red, far.at[z], s2.at[d], r2.at[d], behind[d], chan))
                   for d in range(1, deep)]
            far[z] = red[...]
            return out

        def three():
            last[...] = sum(far[i] for i in range(deep))
            out = [go(remote(last, fin.at[piece(xy)], s3.at[d], r3.at[d], beside[d], chan))
                   for d in range(1, plane)]
            fin[piece(xy)] = last[...]
            return out
        return one, two, three

    def arrive(copies):
        for copy in copies:
            copy.wait_recv()

    a_steps = reduce_steps(0, a_red.shape[0], a_near, a_red, a_far, a_last,
                           (a1s, a1r, a2s, a2r, a3s, a3r))
    b_steps = reduce_steps(2 * kinds * cl, b_red.shape[0], b_near, b_red, b_far, b_last,
                           (b1s, b1r, b2s, b2r, b3s, b3r))
    for h in range(heads):
        mine, rim = head(k, 0, h), head(k, 1, h)
        put(0, h, nt(jnp.concatenate([mine, rim, mine, rim], axis=1),
                     jnp.concatenate([p[h], p[2 * heads + h]], axis=1)))
    for d in range(2):
        rims[d].wait_recv()

        def write(row, r, x, d=d):
            pr[row, HALO * d + r:HALO * d + r + strip, halves[d]] = x
        spread_out(xs.at[d], slot_rim.at[d], write)
    for h in range(heads):
        mine, rim = head(q, 0, h), head(q, 1, h)
        lo = 2 * heads + h
        put(1, h, nn(jnp.concatenate([mine, rim, mine, rim], axis=1),
                     jnp.concatenate([p[h, :, 0:atoms], pr[h], p[lo, :, 0:atoms], pr[lo]], axis=0)))
    weight_terms(0, 0, 2 * cl)
    copies_a = a_steps[0]()
    for h in range(heads):
        mine = head(cx, 0, h)
        hi, lo = heads + h, 3 * heads + h
        inner = nn(jnp.concatenate([mine, mine], axis=1),
                   jnp.concatenate([p[hi, :, 0:atoms], p[lo, :, 0:atoms]], axis=0))
        part[:, 16 * h:16 * h + 16, :] = inner.reshape(M, 16, atoms)
    for h in range(heads):
        arrive(late[2 * h:2 * h + 2])
        rim = head(cx, 1, h)
        hi, lo = heads + h, 3 * heads + h
        outer = nn(jnp.concatenate([rim, rim], axis=1),
                   jnp.concatenate([pr[hi], pr[lo]], axis=0))
        put(2, h, outer + part[:, 16 * h:16 * h + 16, :].reshape(16 * M, atoms))
        if h == heads - 2:
            weight_terms(2, 0, 16 * (heads - 1))
    weight_terms(2, 16 * (heads - 1), cl)
    copies_b = b_steps[0]()
    arrive(copies_a)
    copies_a = a_steps[1]()

    def feature_terms(i):
        for u in range(STEP):
            m = STEP * i + u
            part[m] = nn(wc[math.isqrt(m)], g[m])
        return go(remote(part.at[chunk(i), theirs, :], arrived.at[chunk(i)],
                         ms.at[i], mr.at[i], me, other))

    swap = [feature_terms(i) for i in range(ROUNDS)]
    arrive(copies_b)
    copies_b = b_steps[1]()
    arrive(copies_a)
    copies_a = a_steps[2]()
    for i in range(2):
        swap[i].wait_recv()
    arrive(copies_b)
    copies_b = b_steps[2]()
    outs = []
    for i in range(ROUNDS):
        if i > 1:
            swap[i].wait_recv()
        for u in range(STEP):
            m = STEP * i + u
            gf[m] = (part[m, rows, :] + arrived[m]).astype(bf16)
        outs.append(pltpu.make_async_copy(gf.at[chunk(i)], gf_out.at[chunk(i)], out_sem.at[i]))
        outs[i].start()
    arrive(copies_a)
    split = 2 * kinds * cl
    for n, (copies, at) in enumerate(((copies_a, pl.ds(0, split)),
                                      (copies_b, pl.ds(split, gw_out.shape[0] - split)))):
        if n:
            arrive(copies)
        outs.append(pltpu.make_async_copy(fin.at[at], gw_out.at[at], out_sem.at[ROUNDS + n]))
        outs[-1].start()
    for copy in sent + queue[2 * ROUNDS:]:
        copy.wait_send()
    for copy in outs:
        copy.wait()


def pass_on(*refs):
    n = (len(refs) - 1) // 3
    src, dst, held, sem = refs[:n], refs[n:2 * n], refs[2 * n:3 * n], refs[-1]
    pieces = []
    for a, b, c in zip(src, dst, held):
        cut = a.shape[0] // ROUNDS if a.shape[0] % ROUNDS == 0 else a.shape[0]
        for i in range(0, a.shape[0], cut):
            at = pl.ds(i, cut)
            pieces.append((a.at[at], b.at[at], c.at[at]))
    ins = [pltpu.make_async_copy(a, c, sem.at[0, i]) for i, (a, _, c) in enumerate(pieces)]
    outs = [pltpu.make_async_copy(c, b, sem.at[1, i]) for i, (_, b, c) in enumerate(pieces)]
    for copy in ins:
        copy.start()
    for one, two in zip(ins, outs):
        one.wait()
        two.start()
    for copy in outs:
        copy.wait()


def on_device(features, weights, cotangent, edge_bias, neighbours, valid_mask):
    cl, _, atoms = features.shape
    heads, slots, _ = edge_bias.shape
    feat = jnp.transpose(features, (1, 0, 2))
    cot = jnp.transpose(cotangent, (1, 0, 2))
    w = jnp.transpose(weights, (0, 1, 3, 2))
    S = jax.ShapeDtypeStruct
    both = (2, M, cl, atoms)
    wide = atoms + HALO
    kinds = 3 * (LMAX + 1) * cl
    plane = 16
    deep = lax.axis_size("atom") // plane
    third = (LMAX + 1) * cl
    b_size = -(-third // (8 * plane)) * 8
    V = pltpu.VMEM
    a_row, b_row = (2 * third // plane, 2 * cl), (b_size, 2 * cl)
    padded = (2 * third + plane * b_size, 2 * cl)
    gf, total, grad_bias = pl.pallas_call(
        functools.partial(layer_kernel, plane),
        out_shape=(S((M, cl, atoms), bf16), S((kinds, 2 * cl), f32), S(edge_bias.shape, f32)),
        in_specs=[ANY, ANY, VMEM, VMEM, VMEM, VMEM],
        out_specs=(ANY, ANY, VMEM),
        scratch_shapes=[
            V((2, M, 2 * cl, atoms), bf16), V(both, bf16), V(both, bf16), V(both, bf16),
            V(both, bf16), V((2 * heads, atoms, wide), f32), V((2, slots, HALO), jnp.int32),
            V((atoms, HALO), f32), V((2, HALO, HALO), f32),
            V((3, atoms, HALO), jnp.int32), V((2, HALO, HALO), jnp.int32),
            V((4 * heads, atoms, wide + HALO), bf16), V((4 * heads, atoms, atoms), bf16),
            V((M, 3 * cl, atoms), bf16), V((M, 2 * cl, atoms), f32), V((M, cl, atoms), f32),
            V((M, cl, atoms), bf16), V((LMAX + 1, 2 * cl, 3 * cl), bf16), V(padded, f32),
            V((plane, *a_row), f32), V(a_row, f32), V((deep, *a_row), f32), V(a_row, f32),
            V((plane, *b_row), f32), V(b_row, f32), V((deep, *b_row), f32), V(b_row, f32),
            V(padded, f32),
            DMA((2,)), DMA((ROUNDS + 2,)), DMA((2,)), DMA((2,)), DMA((ROUNDS,)), DMA((ROUNDS,)),
            DMA((2, ROUNDS)), DMA((2, ROUNDS)), DMA((2, ROUNDS)), DMA((2, ROUNDS)),
            DMA((2, heads)), DMA((2, heads)), DMA((2,)), DMA((2,)), DMA((ROUNDS,)), DMA((ROUNDS,)),
            DMA((plane,)), DMA((plane,)), DMA((deep,)), DMA((deep,)), DMA((plane,)), DMA((plane,)),
            DMA((plane,)), DMA((plane,)), DMA((deep,)), DMA((deep,)), DMA((plane,)), DMA((plane,))],
        compiler_params=pltpu.CompilerParams(
            vmem_limit_bytes=62 * 1024 * 1024, collective_id=0, has_side_effects=True),
        name="layer",
    )(feat, cot, w, edge_bias, neighbours, valid_mask)
    results = (gf, total.reshape(3 * (LMAX + 1), cl, 2 * cl), grad_bias)
    gf, total, grad_bias = pl.pallas_call(
        pass_on,
        out_shape=tuple(S(x.shape, x.dtype) for x in results),
        in_specs=[ANY] * 3,
        out_specs=(ANY,) * 3,
        scratch_shapes=[*(V(x.shape, x.dtype) for x in results), DMA((2, 2 * ROUNDS + 1))],
        compiler_params=pltpu.CompilerParams(vmem_limit_bytes=62 * 1024 * 1024),
        name="pass_on",
    )(*results)
    grad_weights = jnp.transpose(total.reshape(3, LMAX + 1, cl, 2 * cl), (0, 1, 3, 2))
    return jnp.transpose(gf, (1, 0, 2)), grad_weights, grad_bias


def solution(mesh):
    return jax.shard_map(
        on_device,
        mesh=mesh,
        in_specs=(P("chan", None, "atom"), P(None, None, None, "chan"), P("chan", None, "atom"),
                  P("chan", None, "atom"), P(None, "atom"), P(None, "atom")),
        out_specs=(P("chan", None, "atom"), P(None, None, None, "chan"), P("chan", None, "atom")),
        check_vma=False,
    )
```
